128 devices in a mesh: fibre: 32 (over y, z_lo, x), band: 4 (over z_hi, core).
Axes of the slice: x: 4, y: 4, z: 4 (z_hi: 2, z_lo: 2; z = z_hi * 2 + z_lo), core: 2. Of those that a mesh axis runs over, the one named last changes fastest.
Arguments:
- traces: bfloat16 [4096, 8192], P('fibre', 'band'), may hold values from -6 to 6
- alive: int32 [4096], P('fibre'), may hold values 0 or 1
- reach: int32 [4096], P('fibre'), may hold values from 1 to 128, as said below
Outputs:
- correlation: bfloat16 [128, 4096, 512], P(('fibre', 'band'))
The draws below stay inside these ranges and needn't reach their ends.
Inputs may be any that keep to these rules, and one draw needn't show every extreme that they name: `reach`: each value is an offset limit of one channel; both 1 and 128 occur in every draw.
All inputs are finite; a program needn't handle non-finite values. No bound on the sum of `alive` on one device may be relied on, other than what follows from the above.
Results may differ from the reference program's by a relative error of at most 0.015.
Values may be sent and summed in bfloat16 or wider, within the bound.
No kernel may reach another device: no remote copies, remote signals or barrier semaphores. Data moves between devices by JAX's collectives and lax.ppermute only.
A program may use at most 192 MiB of HBM per device.

```python
import math
import jax
import jax.numpy as jnp
from jax import lax

NT = 8192
NF = 1024
HW = 32
OFFS = 128
LAGS = 512
CHANNELS = 4096


def draw_reach(key, part):
    values = jax.random.randint(jax.random.fold_in(key, 11), (CHANNELS,), 1, OFFS + 1, dtype=jnp.int32)
    top_spot = jax.random.randint(jax.random.fold_in(key, 12), (), 0, CHANNELS, dtype=jnp.int32)
    low_spot = (top_spot + 1 + jax.random.randint(jax.random.fold_in(key, 13), (), 0, CHANNELS - 1, dtype=jnp.int32)) % CHANNELS
    positions = jnp.arange(CHANNELS, dtype=jnp.int32)
    values = jnp.where(positions == top_spot, OFFS, values)
    values = jnp.where(positions == low_spot, 1, values)
    return values.astype(jnp.int32)


def set_ends(result, stream_key, least, top_value):
    longest = result.shape.index(max(result.shape))
    spots = []
    for shift in (0, 1):
        where = [jax.random.randint(jax.random.fold_in(stream_key, axis), (), 0, length) for axis, length in enumerate(result.shape)]
        where[longest] = (where[longest] + shift) % result.shape[longest]
        spots.append(tuple(where))
    return result.at[spots[0]].set(least).at[spots[1]].set(top_value)


def block_scale(stream_key, shape, split, least, high):
    loudness, own = 1.0, jax.random.fold_in(stream_key, 6)
    for dim, blocks in split:
        steps = jnp.exp(jax.random.uniform(jax.random.fold_in(own, dim), (blocks,), jnp.float32, least / len(split), high / len(split)))
        loudness = loudness * jnp.repeat(steps, shape[dim] // blocks).reshape([-1 if axis == dim else 1 for axis in range(len(shape))])
    return loudness


def normal_values(stream_key, shape, scale, most, pieces=(), kind=jnp.bfloat16):
    factor_of = block_scale(stream_key, shape, pieces, -0.22, 0.18) if pieces else 1.0
    array = jax.random.normal(stream_key, shape, jnp.float32) * scale * factor_of
    return jnp.minimum(jnp.maximum(array, -most), most).astype(kind)


def setup_inputs(seed: int = 0) -> dict:
    key_list = jax.random.split(jax.random.key(seed), 4)
    traces = normal_values(key_list[0], (CHANNELS, NT), 1.0, 6.0, ((0, 32), (1, 4)))
    alive = set_ends((jax.random.randint(key_list[1], (CHANNELS,), 0, 8) < 7).astype(jnp.int32), jax.random.fold_in(key_list[1], 1), 0, 1)
    reach = draw_reach(jax.random.fold_in(key_list[3], 71), 0)
    return {"traces": traces, "alive": alive, "reach": reach}


epsilon = 1e-06

def trig_angles(freq_index, sample_index):
    phase = freq_index[:, None] * sample_index[None, :] % NT
    return phase.astype(jnp.float32) * (2.0 * math.pi / NT)

def lag_table():
    freq_index = jnp.arange(NF, dtype=jnp.int32)
    lag_index = ((jnp.arange(LAGS, dtype=jnp.int32) - LAGS // 2) % NT).astype(jnp.int32)
    angles = trig_angles(freq_index, lag_index)
    weights = jnp.where(freq_index == 0, 1.0, 2.0).astype(jnp.float32)[:, None]
    stacked = jnp.stack([weights * jnp.cos(angles), -weights * jnp.sin(angles)], axis=1)
    return stacked.reshape(2 * NF, LAGS).astype(jnp.bfloat16)

def window_matrix(row_total):
    row_index = jnp.arange(row_total, dtype=jnp.int32)[:, None]
    col_index = jnp.arange(row_total + 2 * HW, dtype=jnp.int32)[None, :]
    spread = col_index - row_index
    return ((spread >= 0) & (spread <= 2 * HW)).astype(jnp.float32)

def reference(traces, alive, reach):
    channel_count = traces.shape[0]
    freq_index = jnp.arange(NF, dtype=jnp.int32)
    sample_index = jnp.arange(NT, dtype=jnp.int32)
    angles = trig_angles(freq_index, sample_index)
    trig_table = jnp.stack([jnp.cos(angles), -jnp.sin(angles)], axis=1).reshape(2 * NF, NT).astype(jnp.bfloat16)
    spectrum = lax.dot_general(trig_table, traces, (((1,), (1,)), ((), ())), preferred_element_type=jnp.float32)
    spectrum = spectrum.reshape(NF, 2, channel_count)
    spec_power = spectrum[:, 0] * spectrum[:, 0] + spectrum[:, 1] * spectrum[:, 1]
    padded = jnp.pad(spec_power, ((HW, HW), (0, 0)))
    window_sum = jnp.dot(window_matrix(NF), padded, precision=lax.Precision.HIGHEST)
    counts = (jnp.minimum(freq_index + HW, NF - 1) - jnp.maximum(freq_index - HW, 0) + 1).astype(jnp.float32)
    scale = alive.astype(jnp.float32)[None, :] / jnp.sqrt(window_sum / counts[:, None] + epsilon)
    whitened = (spectrum * scale[:, None, :]).astype(jnp.bfloat16)
    extended = jnp.concatenate([whitened, jnp.zeros((NF, 2, OFFS), jnp.bfloat16)], axis=2)
    first = whitened.astype(jnp.float32)
    reach_values = reach.astype(jnp.float32)
    lag_basis = lag_table()

    def one_offset(offset):
        partner = lax.dynamic_slice_in_dim(extended, (offset + 1).astype(jnp.int32), channel_count, 2).astype(jnp.float32)
        keep_mask = ((offset + 1).astype(jnp.float32) <= reach_values).astype(jnp.float32)
        real_part = (first[:, 0] * partner[:, 0] + first[:, 1] * partner[:, 1]) * keep_mask
        imag_part = (first[:, 1] * partner[:, 0] - first[:, 0] * partner[:, 1]) * keep_mask
        cross_spec = jnp.stack([real_part, imag_part], axis=1).astype(jnp.bfloat16).reshape(2 * NF, channel_count)
        lagged = lax.dot_general(cross_spec, lag_basis, (((0,), (0,)), ((), ())), preferred_element_type=jnp.float32)
        return (lagged * (1.0 / math.sqrt(NF))).astype(jnp.bfloat16)
    return lax.map(one_offset, jnp.arange(OFFS, dtype=jnp.int32))
```

```python
import math

import jax
import jax.numpy as jnp
import ml_dtypes
import numpy as np
from jax import lax
from jax.experimental import pallas as pl
from jax.experimental.pallas import tpu as pltpu
from jax.sharding import PartitionSpec as P

NT = 8192
NF = 1024
HW = 32
OFFS = 128
LAGS = 512
TURNS = 4
QUART = NT // TURNS
SUB = NF // TURNS
HALF = LAGS // 2
LANE = 128
epsilon = 1e-06
ALL = ("fibre", "band")


def bins():
    return np.arange(TURNS)[:, None] + TURNS * np.arange(SUB)[None, :]


def dft_table():
    phase = np.arange(QUART, dtype=np.int64)[:, None, None] * bins()[None] % NT
    angles = phase * (2.0 * math.pi / NT)
    table = np.stack([np.cos(angles), -np.sin(angles)], axis=2)
    return table.reshape(QUART, 2 * NF).astype(ml_dtypes.bfloat16)


def window_bands():
    gap = np.arange(SUB)[:, None] - np.arange(SUB)[None, :]
    reach = HW // TURNS
    same = np.abs(gap) <= reach
    later = (gap >= -reach) & (gap < reach)
    earlier = (gap > -reach) & (gap <= reach)
    return np.stack([same, later, earlier]).astype(ml_dtypes.bfloat16)


def window_counts():
    k = bins()
    counts = np.minimum(k + HW, NF - 1) - np.maximum(k - HW, 0) + 1
    return (1.0 / counts).astype(np.float32).reshape(TURNS, 1, SUB)


def half_sample():
    angle = bins().reshape(1, NF) * (math.pi / NT)
    return np.stack([np.cos(angle), np.sin(angle)]).astype(np.float32)


def lag_tables():
    k = bins().reshape(NF, 1)
    angle = k * (np.arange(HALF)[None, :] + 0.5) * (2.0 * math.pi / NT)
    weight = np.where(k == 0, 1.0, 2.0) / math.sqrt(NF)
    return np.stack([weight * np.cos(angle), weight * np.sin(angle)]).astype(ml_dtypes.bfloat16)


def flip_matrix():
    return np.eye(HALF)[::-1].astype(ml_dtypes.bfloat16)


def own_column(row, first, rows):
    shape = (rows, row.shape[1])
    lane = lax.broadcasted_iota(jnp.int32, shape, 1)
    line = lax.broadcasted_iota(jnp.int32, shape, 0)
    picked = jnp.where(lane == line + first, jnp.broadcast_to(row, shape), 0.0)
    return jnp.sum(picked, axis=1, keepdims=True)


def bf16_terms(values):
    high = values.astype(jnp.bfloat16)
    rest = values - high.astype(jnp.float32)
    middle = rest.astype(jnp.bfloat16)
    low = (rest - middle.astype(jnp.float32)).astype(jnp.bfloat16)
    return high, middle, low


def exact_dot(values, table):
    total = None
    for term in bf16_terms(values):
        part = jnp.dot(term, table, preferred_element_type=jnp.float32)
        total = part if total is None else total + part
    return total


def whiten_kernel(rank_ref, x_ref, table_ref, bands_ref, counts_ref, alive_ref, out_ref):
    own = x_ref.shape[0] // TURNS
    x = x_ref[...]
    real, imag = [], []
    for m in range(TURNS):
        prod = jnp.dot(
            x, table_ref[:, pl.ds(m * 2 * SUB, 2 * SUB)], preferred_element_type=jnp.float32
        )
        re, im = None, None
        for b in range(TURNS):
            cos_part = prod[b * own : (b + 1) * own, :SUB]
            sin_part = prod[b * own : (b + 1) * own, SUB:]
            turn = b * m % TURNS
            add_re = (cos_part, sin_part, -cos_part, -sin_part)[turn]
            add_im = (sin_part, -cos_part, -sin_part, cos_part)[turn]
            re = add_re if re is None else re + add_re
            im = add_im if im is None else im + add_im
        real.append(re)
        imag.append(im)
    power = [re * re + im * im for re, im in zip(real, imag)]
    alive = own_column(alive_ref[...].astype(jnp.float32), rank_ref[0] * own, own)
    after, before = [None] * TURNS, [None] * TURNS
    for m in range(1, TURNS):
        before[m] = power[m - 1] if m == 1 else before[m - 1] + power[m - 1]
    for m in range(TURNS - 2, -1, -1):
        after[m] = power[m + 1] if m == TURNS - 2 else after[m + 1] + power[m + 1]
    same = exact_dot(jnp.concatenate(power), bands_ref[0])
    later = exact_dot(jnp.concatenate(after[:-1]), bands_ref[1])
    earlier = exact_dot(jnp.concatenate(before[1:]), bands_ref[2])
    for m in range(TURNS):
        total = same[m * own : (m + 1) * own]
        if m < TURNS - 1:
            total = total + later[m * own : (m + 1) * own]
        if m > 0:
            total = total + earlier[(m - 1) * own : m * own]
        scale = alive / jnp.sqrt(total * counts_ref[m] + epsilon)
        out_ref[:, pl.ds(m * SUB, SUB)] = (real[m] * scale).astype(out_ref.dtype)
        out_ref[:, pl.ds(NF + m * SUB, SUB)] = (imag[m] * scale).astype(out_ref.dtype)


def whitened_spectra(rank, x, alive):
    own = x.shape[0] // TURNS
    smem = pl.BlockSpec(memory_space=pltpu.SMEM)
    vmem = pl.BlockSpec(memory_space=pltpu.VMEM)
    return pl.pallas_call(
        whiten_kernel,
        out_shape=jax.ShapeDtypeStruct((own, 2 * NF), jnp.bfloat16),
        in_specs=[smem] + [vmem] * 5,
        out_specs=vmem,
        compiler_params=pltpu.CompilerParams(vmem_limit_bytes=32 << 20),
        name="whiten",
    )(
        rank,
        x,
        jnp.asarray(dft_table()),
        jnp.asarray(window_bands()),
        jnp.asarray(window_counts()),
        alive,
    )


STEP = 16


def lag_kernel(*refs):
    rank_ref, *piece_refs = refs[:6]
    reach_ref, shift_ref, basis_ref, flip_ref, out_ref, a_ref, b_ref, c_ref = refs[6:]
    own = piece_refs[0].shape[0]
    tiles = NF // LANE
    step = pl.program_id(0)

    @pl.when(step == 0)
    def _():
        for p, piece in enumerate(piece_refs):
            for j in range(2 * tiles):
                part = piece[:, pl.ds(j * LANE, LANE)].astype(jnp.float32)
                b_ref[j, pl.ds(p * own, own), :] = part
        for j in range(tiles):
            re = b_ref[j, pl.ds(0, own), :]
            im = b_ref[tiles + j, pl.ds(0, own), :]
            cos = shift_ref[0, :, pl.ds(j * LANE, LANE)]
            sin = shift_ref[1, :, pl.ds(j * LANE, LANE)]
            a_ref[j] = re * cos + im * sin
            a_ref[tiles + j] = im * cos - re * sin

    first = step * STEP
    for j in range(tiles):
        a_re, a_im = a_ref[j], a_ref[tiles + j]
        for i in range(STEP):
            b_re = b_ref[j, pl.ds(first + i + 1, own), :]
            b_im = b_ref[tiles + j, pl.ds(first + i + 1, own), :]
            rows, lanes = pl.ds(i * own, own), pl.ds(j * LANE, LANE)
            c_ref[0, rows, lanes] = (a_re * b_re + a_im * b_im).astype(jnp.bfloat16)
            c_ref[1, rows, lanes] = (a_im * b_re - a_re * b_im).astype(jnp.bfloat16)
    even = jnp.dot(c_ref[0], basis_ref[0], preferred_element_type=jnp.float32)
    odd = jnp.dot(c_ref[1], basis_ref[1], preferred_element_type=jnp.float32)
    reach = own_column(reach_ref[...].astype(jnp.float32), rank_ref[0] * own, own)
    keep = jnp.concatenate([reach >= (first + i + 1).astype(jnp.float32) for i in range(STEP)])
    keep = jnp.broadcast_to(keep, even.shape)
    ahead = jnp.where(keep, even - odd, 0.0).astype(jnp.bfloat16)
    behind = jnp.where(keep, even + odd, 0.0).astype(jnp.bfloat16)
    behind = jnp.dot(behind, flip_ref[...], preferred_element_type=jnp.float32).astype(jnp.bfloat16)
    out_ref[:, :, pl.ds(0, HALF)] = behind.reshape(STEP, own, HALF)
    out_ref[:, :, pl.ds(HALF, HALF)] = ahead.reshape(STEP, own, HALF)


def lag_correlations(rank, pieces, reach):
    own = pieces[0].shape[0]
    vmem = pl.BlockSpec(memory_space=pltpu.VMEM)
    return pl.pallas_call(
        lag_kernel,
        out_shape=jax.ShapeDtypeStruct((OFFS, own, LAGS), jnp.bfloat16),
        grid=(OFFS // STEP,),
        in_specs=[pl.BlockSpec(memory_space=pltpu.SMEM)] + [vmem] * 9,
        out_specs=pl.BlockSpec((STEP, own, LAGS), lambda i: (i, 0, 0)),
        scratch_shapes=[
            pltpu.VMEM((2 * NF // LANE, own, LANE), jnp.float32),
            pltpu.VMEM((2 * NF // LANE, len(pieces) * own, LANE), jnp.float32),
            pltpu.VMEM((2, STEP * own, NF), jnp.bfloat16),
        ],
        compiler_params=pltpu.CompilerParams(vmem_limit_bytes=32 << 20),
        name="lags",
    )(
        rank,
        *pieces,
        reach,
        jnp.asarray(half_sample()),
        jnp.asarray(lag_tables()),
        jnp.asarray(flip_matrix()),
    )


def on_device(traces, alive, reach):
    channels, samples = traces.shape
    bands = lax.axis_size("band")
    count = lax.axis_size("fibre") * bands
    own = channels // bands
    rank = lax.axis_index("band").astype(jnp.int32).reshape(1)
    quarters = lax.all_to_all(
        traces.reshape(bands, own, samples), "band", split_axis=0, concat_axis=0, tiled=True
    )
    whitened = whitened_spectra(
        rank, quarters.reshape(channels, samples), alive.reshape(1, channels)
    )
    pieces = [whitened] + [
        lax.ppermute(whitened, ALL, [(i + j, i) for i in range(count - j)])
        for j in range(1, OFFS // own + 1)
    ]
    lagged = lag_correlations(rank, pieces, reach.reshape(1, channels))
    return lax.all_to_all(lagged, ALL, split_axis=0, concat_axis=1, tiled=True)


def solution(mesh):
    return jax.shard_map(
        on_device,
        mesh=mesh,
        in_specs=(P("fibre", "band"), P("fibre"), P("fibre")),
        out_specs=P(ALL, None, None),
        check_vma=False,
    )
```

```python
import math

import jax
import jax.numpy as jnp
import ml_dtypes
import numpy as np
from jax import lax
from jax.experimental import pallas as pl
from jax.experimental.pallas import tpu as pltpu
from jax.sharding import PartitionSpec as P

NT = 8192
NF = 1024
HW = 32
OFFS = 128
LAGS = 512
TURNS = 4
QUART = NT // TURNS
SUB = NF // TURNS
LANE = 128
COEFS = 160
GROUPS = LANE // (COEFS - LANE)
CORES = 2
epsilon = 1e-06
ALL = ("fibre", "band")


def bins():
    return np.arange(TURNS)[:, None] + TURNS * np.arange(SUB)[None, :]


def dft_table():
    phase = np.arange(QUART, dtype=np.int64)[:, None, None] * bins()[None] % NT
    angles = phase * (2.0 * math.pi / NT)
    table = np.stack([np.cos(angles), -np.sin(angles)], axis=2)
    return table.reshape(QUART, 2 * NF).astype(ml_dtypes.bfloat16)


def window_bands():
    gap = np.arange(SUB)[:, None] - np.arange(SUB)[None, :]
    reach = HW // TURNS
    same = np.abs(gap) <= reach
    later = (gap >= -reach) & (gap < reach)
    earlier = (gap > -reach) & (gap <= reach)
    return np.stack([same, later, earlier]).astype(ml_dtypes.bfloat16)


def window_counts():
    k = bins()
    counts = np.minimum(k + HW, NF - 1) - np.maximum(k - HW, 0) + 1
    return (1.0 / counts).astype(np.float32).reshape(TURNS, 1, SUB)


def lag_vectors():
    n = np.arange(LAGS)
    width = NF / NT
    diagonal = ((LAGS - 1 - 2 * n) / 2.0) ** 2 * math.cos(2 * math.pi * width)
    beside = n[1:] * (LAGS - n[1:]) / 2.0
    matrix = np.diag(diagonal) + np.diag(beside, 1) + np.diag(beside, -1)
    vectors = np.linalg.eigh(matrix)[1][:, ::-1][:, :COEFS].T
    return vectors * np.where(vectors[:, LAGS // 2] < 0, -1.0, 1.0)[:, None]


def repeated(table):
    return np.concatenate([table[:, :LANE]] + [table[:, LANE:]] * GROUPS, axis=1)


def lag_tables():
    k = bins().reshape(NF, 1)
    angle = k * (np.arange(LAGS)[None, :] - LAGS // 2) * (2.0 * math.pi / NT)
    weight = np.where(k == 0, 1.0, 2.0) / math.sqrt(NF)
    table = np.concatenate([weight * np.cos(angle), -weight * np.sin(angle)])
    vectors = lag_vectors()
    project = repeated(table @ vectors.T)
    expand = repeated(vectors.T).T
    return project.astype(ml_dtypes.bfloat16), expand.astype(ml_dtypes.bfloat16)


def own_column(row, first, rows):
    shape = (rows, row.shape[1])
    lane = lax.broadcasted_iota(jnp.int32, shape, 1)
    line = lax.broadcasted_iota(jnp.int32, shape, 0)
    picked = jnp.where(lane == line + first, jnp.broadcast_to(row, shape), 0.0)
    return jnp.sum(picked, axis=1, keepdims=True)


def bf16_terms(values):
    high = values.astype(jnp.bfloat16)
    rest = values - high.astype(jnp.float32)
    middle = rest.astype(jnp.bfloat16)
    low = (rest - middle.astype(jnp.float32)).astype(jnp.bfloat16)
    return high, middle, low


def exact_dot(values, table):
    total = None
    for term in bf16_terms(values):
        part = jnp.dot(term, table, preferred_element_type=jnp.float32)
        total = part if total is None else total + part
    return total


def whiten_kernel(rank_ref, x_ref, table_ref, bands_ref, counts_ref, alive_ref, out_ref):
    own = x_ref.shape[0] // TURNS
    x = x_ref[...]
    real, imag = [], []
    for m in range(TURNS):
        prod = jnp.dot(
            x, table_ref[:, pl.ds(m * 2 * SUB, 2 * SUB)], preferred_element_type=jnp.float32
        )
        re, im = None, None
        for b in range(TURNS):
            cos_part = prod[b * own : (b + 1) * own, :SUB]
            sin_part = prod[b * own : (b + 1) * own, SUB:]
            turn = b * m % TURNS
            add_re = (cos_part, sin_part, -cos_part, -sin_part)[turn]
            add_im = (sin_part, -cos_part, -sin_part, cos_part)[turn]
            re = add_re if re is None else re + add_re
            im = add_im if im is None else im + add_im
        real.append(re)
        imag.append(im)
    power = [re * re + im * im for re, im in zip(real, imag)]
    alive = own_column(alive_ref[...].astype(jnp.float32), rank_ref[0] * own, own)
    after, before = [None] * TURNS, [None] * TURNS
    for m in range(1, TURNS):
        before[m] = power[m - 1] if m == 1 else before[m - 1] + power[m - 1]
    for m in range(TURNS - 2, -1, -1):
        after[m] = power[m + 1] if m == TURNS - 2 else after[m + 1] + power[m + 1]
    same = exact_dot(jnp.concatenate(power), bands_ref[0])
    later = exact_dot(jnp.concatenate(after[:-1]), bands_ref[1])
    earlier = exact_dot(jnp.concatenate(before[1:]), bands_ref[2])
    for m in range(TURNS):
        total = same[m * own : (m + 1) * own]
        if m < TURNS - 1:
            total = total + later[m * own : (m + 1) * own]
        if m > 0:
            total = total + earlier[(m - 1) * own : m * own]
        scale = alive / jnp.sqrt(total * counts_ref[m] + epsilon)
        out_ref[:, pl.ds(m * SUB, SUB)] = (real[m] * scale).astype(out_ref.dtype)
        out_ref[:, pl.ds(NF + m * SUB, SUB)] = (imag[m] * scale).astype(out_ref.dtype)


def whitened_spectra(rank, x, alive):
    own = x.shape[0] // TURNS
    smem = pl.BlockSpec(memory_space=pltpu.SMEM)
    vmem = pl.BlockSpec(memory_space=pltpu.VMEM)
    return pl.pallas_call(
        whiten_kernel,
        out_shape=jax.ShapeDtypeStruct((own, 2 * NF), jnp.bfloat16),
        in_specs=[smem] + [vmem] * 5,
        out_specs=vmem,
        compiler_params=pltpu.CompilerParams(vmem_limit_bytes=32 << 20),
        name="whiten",
    )(
        rank,
        x,
        jnp.asarray(dft_table()),
        jnp.asarray(window_bands()),
        jnp.asarray(window_counts()),
        alive,
    )


STEP = 8


def group_mask(rows):
    lane = lax.broadcasted_iota(jnp.int32, (rows, LANE), 1)
    line = lax.broadcasted_iota(jnp.int32, (rows, LANE), 0)
    return lane // (LANE // GROUPS) == line // (rows // GROUPS)


def lag_kernel(rank_ref, *refs):
    piece_refs, reach_ref, table_ref, out_ref, b_ref, c_ref = refs[:-5], *refs[-5:]
    blocks = len(piece_refs) // CORES
    own = piece_refs[0].shape[0]
    rows = CORES * own
    tiles = 2 * NF // LANE
    step = pl.program_id(0)
    core = rank_ref[0] % CORES

    @pl.when(step == 0)
    def _():
        for p in range(blocks):
            for swap in range(CORES):
                at = p * rows + own * (core + swap - 2 * core * swap)
                for j in range(tiles):
                    part = piece_refs[CORES * p + swap][:, pl.ds(j * LANE, LANE)]
                    b_ref[j, pl.ds(pl.multiple_of(at, own), own), :] = part.astype(jnp.float32)

    first = CORES * STEP * step + core + 1
    for j in range(tiles // 2):
        a_re, a_im = b_ref[j, pl.ds(0, rows), :], b_ref[tiles // 2 + j, pl.ds(0, rows), :]
        for i in range(STEP):
            near = pl.ds(first + CORES * i, rows)
            b_re, b_im = b_ref[j, near, :], b_ref[tiles // 2 + j, near, :]
            line = pl.ds(i * rows, rows)
            c_ref[line, pl.ds(j * LANE, LANE)] = (a_re * b_re + a_im * b_im).astype(jnp.bfloat16)
            c_ref[line, pl.ds(NF + j * LANE, LANE)] = (a_im * b_re - a_re * b_im).astype(
                jnp.bfloat16
            )
    coefs = jnp.dot(c_ref[...], table_ref[...], preferred_element_type=jnp.float32)
    reach = own_column(
        reach_ref[...].astype(jnp.float32), rank_ref[0] // CORES * rows, rows
    )
    member = group_mask(rows)
    for i in range(STEP):
        part = coefs[i * rows : (i + 1) * rows]
        keep = jnp.broadcast_to(reach, (rows, LANE)) >= (first + CORES * i).astype(jnp.float32)
        out_ref[i, pl.ds(0, rows), :] = jnp.where(keep, part[:, :LANE], 0.0).astype(jnp.bfloat16)
        rest = jnp.where(keep & member, part[:, LANE:], 0.0)
        rest = jnp.sum(rest.reshape(GROUPS, rows // GROUPS, LANE), axis=0)
        out_ref[i, pl.ds(rows, rows // GROUPS), :] = rest.astype(jnp.bfloat16)


def lag_coefficients(rank, pieces, reach, table):
    own = pieces[0].shape[0]
    rows = CORES * own
    offsets = OFFS // CORES
    packed = rows + rows // GROUPS
    vmem = pl.BlockSpec(memory_space=pltpu.VMEM)
    return pl.pallas_call(
        lag_kernel,
        out_shape=jax.ShapeDtypeStruct((offsets, packed, LANE), jnp.bfloat16),
        grid=(offsets // STEP,),
        in_specs=[pl.BlockSpec(memory_space=pltpu.SMEM)] + [vmem] * (len(pieces) + 2),
        out_specs=pl.BlockSpec((STEP, packed, LANE), lambda i: (i, 0, 0)),
        scratch_shapes=[
            pltpu.VMEM((2 * NF // LANE, len(pieces) * own, LANE), jnp.float32),
            pltpu.VMEM((STEP * rows, 2 * NF), jnp.bfloat16),
        ],
        compiler_params=pltpu.CompilerParams(vmem_limit_bytes=32 << 20),
        name="lags",
    )(rank, *pieces, reach, table)


def expand_kernel(coefs_ref, table_ref, out_ref):
    count, packed, _ = coefs_ref.shape
    rows = packed * GROUPS // (GROUPS + 1)
    member = group_mask(rows)
    lines = []
    for i in range(count):
        rest = coefs_ref[i, pl.ds(rows, rows // GROUPS), :].astype(jnp.float32)
        rest = jnp.where(member, jnp.concatenate([rest] * GROUPS), 0.0).astype(jnp.bfloat16)
        lines.append(jnp.concatenate([coefs_ref[i, pl.ds(0, rows), :], rest], axis=1))
    lags = jnp.dot(jnp.concatenate(lines), table_ref[...], preferred_element_type=jnp.float32)
    out_ref[0] = lags.astype(out_ref.dtype)


def expanded(coefs, table):
    count, packed, _ = coefs.shape
    rows = packed * GROUPS // (GROUPS + 1)
    return pl.pallas_call(
        expand_kernel,
        out_shape=jax.ShapeDtypeStruct((1, count * rows, LAGS), jnp.bfloat16),
        grid=(count // STEP,),
        in_specs=[
            pl.BlockSpec((STEP, packed, LANE), lambda i: (i, 0, 0)),
            pl.BlockSpec(memory_space=pltpu.VMEM),
        ],
        out_specs=pl.BlockSpec((1, STEP * rows, LAGS), lambda i: (0, i, 0)),
        compiler_params=pltpu.CompilerParams(vmem_limit_bytes=32 << 20),
        name="expand",
    )(coefs, table)


def on_device(traces, alive, reach):
    channels, samples = traces.shape
    bands = lax.axis_size("band")
    count = lax.axis_size("fibre") * bands
    own = channels // bands
    rank = lax.axis_index("band").astype(jnp.int32).reshape(1)
    project, expand = lag_tables()
    quarters = lax.all_to_all(
        traces.reshape(bands, own, samples), "band", split_axis=0, concat_axis=0, tiled=True
    )
    whitened = whitened_spectra(
        rank, quarters.reshape(channels, samples), alive.reshape(1, channels)
    )
    pieces = []
    for chips in range(OFFS // (CORES * own) + 1):
        by = CORES * chips
        pairs = [(i + by, i) for i in range(count - by)]
        piece = lax.ppermute(whitened, ALL, pairs) if by else whitened
        pieces += [piece, lax.ppermute(piece, ALL, [(i ^ 1, i) for i in range(count)])]
    coefs = lag_coefficients(rank, pieces, reach.reshape(1, channels), jnp.asarray(project))
    groups = [list(range(core, count, CORES)) for core in range(CORES)]
    coefs = lax.all_to_all(
        coefs, ALL, split_axis=0, concat_axis=0, axis_index_groups=groups, tiled=True
    )
    return expanded(coefs, jnp.asarray(expand))


def solution(mesh):
    return jax.shard_map(
        on_device,
        mesh=mesh,
        in_specs=(P("fibre", "band"), P("fibre"), P("fibre")),
        out_specs=P(ALL, None, None),
        check_vma=False,
    )
```
